32 devices in a mesh: cells: 8 (over z, y), orb: 4 (over x, core).
Axes of the slice: x: 2, y: 2, z: 4, core: 2. Of those that a mesh axis runs over, the one named last changes fastest.
Arguments:
- orbitals: bfloat16 [1024, 256, 512], P('cells', 'orb'), may hold values from -6 to 6
- gradient_matrix: bfloat16 [512, 1536], replicated, may hold values from -0.25 to 0.25
- quad_weights: float32 [512], replicated, may hold values from 0.0009765625 to 0.00390625
- cell_scale: float32 [1024], P('cells'), may hold values from 0.5 to 2
- occupations: float32 [256], P('orb'), may hold values from 0 to 2
- support_cell: int32 [1024], P('cells'), may hold values from 0 to 1023, as said below
- support_atom: int32 [1024], P('cells'), may hold values from -1 to 63, as said below
- proj_values: bfloat16 [1024, 16, 512], P('cells'), may hold values from -6 to 6
- proj_coupling: float32 [64, 16], replicated, may hold values from -0.6 to 0.6
Outputs:
- eshelby: float32 [6, 1024], P(None, 'cells')
- forces: float32 [3, 64], P(None, 'cells')
The draws below stay inside these ranges and needn't reach their ends.
Inputs may be any that keep to these rules, and one draw needn't show every extreme that they name: `support_cell`: row r lies in the slab of cells from (r // 128) * 128 to that plus 128 - 1. `support_atom`: in each aligned block of 128 rows the live rows (atom 0 or more) come first and padding (-1) after; each such block has 32 or more live rows, and some block is all live. Atom a belongs to slab a // 8; a live row of block s names an atom of a slab (s + d) mod (number of slabs) with d from -2 to 2.
All inputs are finite; a program needn't handle non-finite values.
Results may differ from the reference program's by a relative error of at most 0.0048.
Values sent between devices are 32-bit elements; how exact they have to be, the bound alone decides.
No kernel may reach another device: no remote copies, remote signals or barrier semaphores. Data moves between devices by JAX's collectives and lax.ppermute only.
A program may use at most 192 MiB of HBM per device.

```python
import math
import jax
import jax.numpy as jnp
from jax import lax

NODES = 512
NORB = 256
NPROJ = 16
BLOCK = 128
REACH = 2
CELL_DEV = 128
SUP_DEV = 128
ATOM_DEV = 8
CELLS = 1024
SUPPORT = 1024
ATOMS = 64
N_CELLS = 8


def draw_occupations(key, part):
    position = jnp.arange(NORB).astype(jnp.float32)
    fermi = 2.0 / (1.0 + jnp.exp((position - 0.75 * NORB) / (0.08 * NORB)))
    jitter = jax.random.uniform(key, (NORB,), jnp.float32, 0.7, 1.0)
    return fermi * jitter


def draw_support_cell(key, part):
    slab_count = SUPPORT // SUP_DEV
    offsets = jax.random.randint(jax.random.fold_in(key, 11), (slab_count, SUP_DEV), 0, CELL_DEV)
    base = (jnp.arange(slab_count, dtype=jnp.int32) * CELL_DEV)[:, None]
    return (offsets + base).reshape(SUPPORT).astype(jnp.int32)


def draw_support_atom(key, part):
    slab_count = SUPPORT // SUP_DEV
    seeds = jax.random.split(jax.random.fold_in(key, 23), 6)
    live_rows = SUP_DEV // 4 + jax.random.randint(seeds[0], (slab_count,), 0, SUP_DEV - SUP_DEV // 4 + 1)
    fullest = jax.random.randint(seeds[1], (), 0, slab_count)
    live_rows = jnp.where(jnp.arange(slab_count) == fullest, SUP_DEV, live_rows)
    spread_local = jax.random.randint(seeds[2], (slab_count, SUP_DEV), 0, ATOM_DEV)
    heavy_local = jax.random.randint(seeds[3], (slab_count, SUP_DEV), 0, max(ATOM_DEV // 8, 1))
    picker = jax.random.randint(seeds[4], (slab_count, SUP_DEV), 0, 2)
    local_ids = jnp.where(picker == 1, spread_local, heavy_local)
    offsets = jax.random.randint(seeds[5], (slab_count, SUP_DEV), -REACH, REACH + 1)
    slab_ids = jnp.arange(slab_count, dtype=jnp.int32)[:, None]
    owners = jnp.mod(slab_ids + offsets, slab_count)
    atom_ids = owners * ATOM_DEV + local_ids
    position = jnp.arange(SUP_DEV)[None, :]
    atom_ids = jnp.where(position < live_rows[:, None], atom_ids, -1)
    return atom_ids.reshape(SUPPORT).astype(jnp.int32)


def levels(own_key, dims, pieces, low, largest):
    def one(dim, shards_of):
        steps = jax.random.uniform(jax.random.fold_in(jax.random.fold_in(own_key, 6), dim), (shards_of,), jnp.float32, low / len(pieces), largest / len(pieces))
        return jnp.repeat(jnp.exp(steps), dims[dim] // shards_of).reshape((-1,) + (1,) * (len(dims) - dim - 1))

    level = one(*pieces[0])
    for cut in pieces[1:]:
        level = level * one(*cut)
    return level


def scatter_about(own_key, extent, deviation, bound, cuts=(), kind=jnp.bfloat16):
    entries = deviation * jax.random.normal(own_key, extent, jnp.float32)
    if cuts:
        entries = entries * levels(own_key, extent, cuts, -0.22, 0.18)
    return jnp.clip(entries, -bound, bound).astype(kind)


def setup_inputs(seed: int = 0) -> dict:
    key_of = jax.random.split(jax.random.key(seed), 10)
    return {
        "orbitals": scatter_about(key_of[0], (CELLS, NORB, NODES), 1.0, 6.0, ((0, 8), (1, 4))),
        "gradient_matrix": scatter_about(key_of[1], (NODES, 3 * NODES), NODES ** -0.5, 0.25),
        "quad_weights": jnp.clip(jnp.exp(jax.random.uniform(key_of[2], (NODES,), jnp.float32, math.log(0.0009765625), math.log(0.00390625))), 0.0009765625, 0.00390625),
        "cell_scale": jnp.clip(jnp.exp(math.log(2.0) - 1.3862944 * jax.random.uniform(key_of[3], (CELLS,), jnp.float32) ** levels(key_of[3], (CELLS,), ((0, 8),), -0.2, 0.2)), 0.5, 2.0),
        "occupations": draw_occupations(jax.random.fold_in(key_of[9], 71), 0),
        "support_cell": draw_support_cell(jax.random.fold_in(key_of[9], 71), 0),
        "support_atom": draw_support_atom(jax.random.fold_in(key_of[9], 71), 0),
        "proj_values": scatter_about(key_of[7], (SUPPORT, NPROJ, NODES), 1.0, 6.0, ((0, 8),)),
        "proj_coupling": scatter_about(key_of[8], (ATOMS, NPROJ), 0.1, 0.6, (), jnp.float32),
    }


def stress_terms(gradient, weighting):
    grad_x = gradient[:, :, 0]
    grad_y = gradient[:, :, 1]
    grad_z = gradient[:, :, 2]
    half_square = 0.5 * (grad_x * grad_x + grad_y * grad_y + grad_z * grad_z)
    parts = [half_square - grad_x * grad_x, half_square - grad_y * grad_y, half_square - grad_z * grad_z,
             -grad_x * grad_y, -grad_x * grad_z, -grad_y * grad_z]
    return jnp.stack([jnp.sum(weighting * part, axis=(1, 2)) for part in parts])


def reference(orbitals, gradient_matrix, quad_weights, cell_scale, occupations, support_cell, support_atom, proj_values, proj_coupling):
    weighting_base = occupations[:, None] * quad_weights[None, :] / NORB
    weighted_proj = (quad_weights[None, None, :] * proj_values).astype(jnp.bfloat16)
    atom_range = jnp.arange(ATOMS, dtype=jnp.int32)

    def slab_step(totals, slab_index):
        first_cell = slab_index * CELL_DEV
        slab_orbitals = lax.dynamic_slice_in_dim(orbitals, first_cell, CELL_DEV, 0)
        slab_scales = lax.dynamic_slice_in_dim(cell_scale, first_cell, CELL_DEV, 0)
        gradient = jnp.dot(slab_orbitals.reshape(-1, NODES), gradient_matrix, preferred_element_type=jnp.float32)
        gradient = gradient.reshape(CELL_DEV, NORB, 3, NODES)
        weighting = weighting_base[None] * (slab_scales ** 2)[:, None, None]
        stress = stress_terms(gradient, weighting)
        stored = gradient.astype(jnp.bfloat16)

        def row_step(acc, block_index):
            first_row = slab_index * SUP_DEV + block_index * BLOCK
            cells_here = lax.dynamic_slice_in_dim(support_cell, first_row, BLOCK, 0) - first_cell
            atoms_here = lax.dynamic_slice_in_dim(support_atom, first_row, BLOCK, 0)
            proj_here = lax.dynamic_slice_in_dim(weighted_proj, first_row, BLOCK, 0).astype(jnp.float32)
            scale_here = slab_scales[cells_here]
            picked_orbitals = slab_orbitals[cells_here].astype(jnp.float32)
            picked_grad = stored[cells_here].astype(jnp.float32)
            margin = jnp.einsum("rbq,rnq->rbn", proj_here, picked_orbitals)
            derivative = jnp.einsum("rbq,rniq->ribn", proj_here, picked_grad) * scale_here[:, None, None, None]
            stacked = jnp.concatenate([margin[:, None], derivative], axis=1)
            onehot = (atoms_here[:, None] == atom_range[None, :]).astype(jnp.float32)
            return acc + jnp.einsum("rkbn,ra->kbna", stacked, onehot, precision=lax.Precision.HIGHEST), None

        totals, unused = lax.scan(row_step, totals, jnp.arange(SUP_DEV // BLOCK, dtype=jnp.int32))
        return totals, stress

    initial = jnp.zeros((4, NPROJ, NORB, ATOMS), jnp.float32)
    totals, stress = lax.scan(slab_step, initial, jnp.arange(N_CELLS, dtype=jnp.int32))
    eshelby = jnp.transpose(stress, (1, 0, 2)).reshape(6, CELLS)
    weight_terms = occupations[None, :, None] * jnp.transpose(proj_coupling)[:, None, :]
    forces = -2.0 * jnp.sum(totals[1:] * (totals[0] * weight_terms)[None], axis=(1, 2))
    return eshelby, forces
```

```python
import functools

import jax
import jax.numpy as jnp
from jax import lax
from jax.experimental import pallas as pl
from jax.experimental.pallas import tpu as pltpu
from jax.sharding import PartitionSpec as P

REACH = 2
LANES = 128
PAIRS = ((0, 0), (1, 1), (2, 2), (0, 1), (0, 2), (1, 2))
CONTRACT_LAST = (((1,), (1,)), ((), ()))


def from_behind(shard, axis, by):
    length = lax.axis_size(axis)
    return lax.ppermute(shard, axis, [(i, (i + by) % length) for i in range(length)])


def force_kernel(
    cell_ref,
    window_ref,
    scale_ref,
    weight_ref,
    proj_ref,
    matrix_ref,
    orbitals_hbm,
    *rest,
    window_slabs,
    chunk,
    unroll,
):
    outs = rest[:window_slabs]
    folded, orbitals_ref, acc, sem = rest[window_slabs:]
    rows, parts, projs, nodes = folded.shape
    atoms = outs[0].shape[0]
    orbs = orbitals_ref.shape[1]
    load = pltpu.make_async_copy(orbitals_hbm, orbitals_ref, sem)
    load.start()
    acc[...] = jnp.zeros_like(acc)

    def fold(step, carry):
        at = pl.ds(pl.multiple_of(step * chunk, chunk), chunk)
        scaled = proj_ref[at].astype(jnp.float32) * weight_ref[...][None]
        scaled = scaled.astype(jnp.bfloat16)
        folded[at, 0] = scaled
        flat = scaled.reshape(chunk * projs, nodes)
        for i in range(parts - 1):
            part = lax.dot_general(
                flat,
                matrix_ref[:, i * nodes : (i + 1) * nodes],
                CONTRACT_LAST,
                preferred_element_type=jnp.float32,
            )
            folded[at, i + 1] = part.astype(jnp.bfloat16).reshape(chunk, projs, nodes)
        return carry

    lax.fori_loop(0, rows // chunk, fold, 0)
    load.wait()

    def add_rows(step, carry):
        for j in range(unroll):
            row = step * unroll + j
            cell = cell_ref[row]
            slot = window_ref[row]
            term = lax.dot_general(
                folded[row].reshape(parts * projs, nodes),
                orbitals_ref[cell],
                CONTRACT_LAST,
                preferred_element_type=jnp.float32,
            )
            acc[slot, :projs] += term[:projs]
            acc[slot, projs:] += term[projs:] * scale_ref[cell]
        return carry

    lax.fori_loop(0, rows // unroll, add_rows, 0)
    fold_by = LANES // orbs
    high = parts * projs // fold_by
    for slab in range(window_slabs):
        for atom in range(atoms):
            whole = acc[slab * atoms + atom]
            outs[slab][atom] = jnp.concatenate(
                [whole[k * high : (k + 1) * high] for k in range(fold_by)], axis=1
            )


def window_sums(
    local_cells, window_ids, cell_scale, quad_weights, proj_values, gradient_matrix, orbitals, atoms
):
    rows, projs, nodes = proj_values.shape
    cells, orbs, _ = orbitals.shape
    window_slabs = 2 * REACH + 1
    parts = 1 + gradient_matrix.shape[1] // nodes
    packed = (atoms, parts * projs * orbs // LANES, LANES)
    smem = pl.BlockSpec(memory_space=pltpu.SMEM)
    vmem = pl.BlockSpec(memory_space=pltpu.VMEM)
    flops = 2 * rows * projs * nodes * (nodes * (parts - 1) + orbs * parts)
    return pl.pallas_call(
        functools.partial(force_kernel, window_slabs=window_slabs, chunk=32, unroll=8),
        out_shape=[jax.ShapeDtypeStruct(packed, jnp.float32)] * window_slabs,
        in_specs=[smem, smem, smem, vmem, vmem, vmem, pl.BlockSpec(memory_space=pl.ANY)],
        out_specs=[vmem] * window_slabs,
        scratch_shapes=[
            pltpu.VMEM((rows, parts, projs, nodes), jnp.bfloat16),
            pltpu.VMEM(orbitals.shape, jnp.bfloat16),
            pltpu.VMEM((window_slabs * atoms + 1, parts * projs, orbs), jnp.float32),
            pltpu.SemaphoreType.DMA,
        ],
        cost_estimate=pl.CostEstimate(
            flops=flops, bytes_accessed=2 * orbitals.size + 2 * proj_values.size, transcendentals=0
        ),
        name="window_sums",
    )(
        local_cells,
        window_ids,
        cell_scale,
        quad_weights.reshape(1, nodes),
        proj_values,
        gradient_matrix,
        orbitals,
    )


def stress_kernel(
    weight_ref, scale_ref, matrix_ref, orbitals_ref, out_ref, even, odd, sums, *, block
):
    step = pl.program_id(0)
    orbs, nodes = weight_ref.shape
    cells = out_ref.shape[1]

    def gradient(half, buffer):
        flat = orbitals_ref[half * block : (half + 1) * block].reshape(block * orbs, nodes)
        buffer[...] = jnp.dot(flat, matrix_ref[...], preferred_element_type=jnp.float32)

    def reduce(buffer, first_row):
        totals = [[] for _ in PAIRS]
        for cell in range(block):
            acc = [None] * len(PAIRS)
            for group in range(orbs // 8):
                row = cell * orbs + group * 8
                weight = weight_ref[group * 8 : group * 8 + 8, :]
                grad = [buffer[row : row + 8, i * nodes : (i + 1) * nodes] for i in range(3)]
                scaled = [weight * grad[i] for i in range(3)]
                for k, (i, j) in enumerate(PAIRS):
                    term = scaled[i] * grad[j]
                    acc[k] = term if acc[k] is None else acc[k] + term
            for k in range(len(PAIRS)):
                lanes = acc[k][:, :LANES]
                for c in range(1, nodes // LANES):
                    lanes = lanes + acc[k][:, c * LANES : (c + 1) * LANES]
                totals[k].append(jnp.sum(lanes, axis=0, keepdims=True))
        at = pl.ds(pl.multiple_of(first_row, block), block)
        for k in range(len(PAIRS)):
            sums[k, at, :] = jnp.concatenate(totals[k], axis=0)

    gradient(0, even)
    reduce(odd, 2 * step * block)
    gradient(1, odd)
    reduce(even, (2 * step + 1) * block)

    @pl.when(step == pl.num_programs(0) - 1)
    def finish():
        reduce(odd, cells)
        ones = jnp.ones((8, LANES), jnp.float32)
        whole = [
            lax.dot_general(
                ones,
                sums[k, block:, :],
                CONTRACT_LAST,
                precision=lax.Precision.HIGHEST,
                preferred_element_type=jnp.float32,
            )[:1]
            for k in range(len(PAIRS))
        ]
        half = 0.5 * (whole[0] + whole[1] + whole[2])
        square = scale_ref[...] * scale_ref[...]
        for k in range(3):
            out_ref[k : k + 1, :] = (half - whole[k]) * square
        for k in range(3, 6):
            out_ref[k : k + 1, :] = -whole[k] * square


def stress_sums(weighting, cell_scale, gradient_matrix, orbitals):
    cells, orbs, nodes = orbitals.shape
    block = 512 // orbs
    columns = gradient_matrix.shape[1]
    whole = lambda shape: pl.BlockSpec(shape, lambda t: (0,) * len(shape))
    return pl.pallas_call(
        functools.partial(stress_kernel, block=block),
        grid=(cells // (2 * block),),
        out_shape=jax.ShapeDtypeStruct((6, cells), jnp.float32),
        in_specs=[
            whole((orbs, nodes)),
            whole((1, cells)),
            whole((nodes, columns)),
            pl.BlockSpec((2 * block, orbs, nodes), lambda t: (t, 0, 0)),
        ],
        out_specs=whole((6, cells)),
        scratch_shapes=[
            pltpu.VMEM((block * orbs, columns), jnp.float32),
            pltpu.VMEM((block * orbs, columns), jnp.float32),
            pltpu.VMEM((6, cells + block, LANES), jnp.float32),
        ],
        cost_estimate=pl.CostEstimate(
            flops=2 * orbitals.size * columns, bytes_accessed=2 * orbitals.size, transcendentals=0
        ),
        name="stress_sums",
    )(weighting, cell_scale.reshape(1, cells), gradient_matrix, orbitals)


def local(
    orbitals,
    gradient_matrix,
    quad_weights,
    cell_scale,
    occupations,
    support_cell,
    support_atom,
    proj_values,
    proj_coupling,
):
    cell_count, orbital_count, node_count = orbitals.shape
    proj_count = proj_values.shape[1]
    atom_total = proj_coupling.shape[0]
    slab_total = lax.axis_size("cells")
    atom_share = atom_total // slab_total
    window_slabs = 2 * REACH + 1
    slab_index = lax.axis_index("cells")
    orbital_total = orbital_count * lax.axis_size("orb")

    local_cells = support_cell - slab_index * cell_count
    live_atom = jnp.maximum(support_atom, 0)
    relative = jnp.mod(live_atom // atom_share - slab_index + REACH, slab_total)
    window_ids = relative * atom_share + jnp.mod(live_atom, atom_share)
    window_ids = jnp.where(support_atom >= 0, window_ids, window_slabs * atom_share)

    parts = window_sums(
        local_cells,
        window_ids,
        cell_scale,
        quad_weights,
        proj_values,
        gradient_matrix,
        orbitals,
        atom_share,
    )
    owned = parts[REACH]
    for offset in range(-REACH, REACH + 1):
        if offset != 0:
            owned = owned + from_behind(parts[offset + REACH], "cells", offset)

    weighting = occupations[:, None] * quad_weights[None, :] / orbital_total
    stress_part = stress_sums(weighting, cell_scale, gradient_matrix, orbitals)

    fold_by = LANES // orbital_count
    owned = jnp.concatenate(
        [owned[:, :, k * orbital_count : (k + 1) * orbital_count] for k in range(fold_by)], axis=1
    )
    owned = owned.reshape(atom_share, 4, proj_count, orbital_count)
    coupling = lax.dynamic_slice_in_dim(proj_coupling, slab_index * atom_share, atom_share, 0)
    weight_terms = coupling[:, :, None] * occupations[None, None, :]
    force_part = -2.0 * jnp.sum(owned[:, 1:] * (owned[:, 0] * weight_terms)[:, None], axis=(2, 3))
    eshelby, forces = lax.psum((stress_part, jnp.transpose(force_part)), "orb")
    return (eshelby, forces)


def solution(mesh):
    return jax.shard_map(
        local,
        mesh=mesh,
        in_specs=(
            P("cells", "orb", None),
            P(),
            P(),
            P("cells"),
            P("orb"),
            P("cells"),
            P("cells"),
            P("cells", None, None),
            P(),
        ),
        out_specs=(P(None, "cells"), P(None, "cells")),
        check_vma=False,
    )
```

```python
import functools
import math

import jax
import jax.numpy as jnp
from jax import lax
from jax.experimental import pallas as pl
from jax.experimental.pallas import tpu as pltpu
from jax.sharding import PartitionSpec as P

REACH = 2
LANES = 128
SUBLANES = 8
PAIRS = ((0, 0), (1, 1), (2, 2), (0, 1), (0, 2), (1, 2))
CONTRACT_LAST = (((1,), (1,)), ((), ()))
FORCE_MIB, STRESS_MIB = 28, 30
SMEM = pl.BlockSpec(memory_space=pltpu.SMEM)
VMEM = pl.BlockSpec(memory_space=pltpu.VMEM)
HBM = pl.BlockSpec(memory_space=pltpu.HBM)


def from_behind(shard, axis, by):
    length = lax.axis_size(axis)
    return lax.ppermute(shard, axis, [(i, (i + by) % length) for i in range(length)])


def force_kernel(
    cell_hbm,
    atom_hbm,
    scale_hbm,
    quad_hbm,
    proj_hbm,
    matrix_hbm,
    orbitals_hbm,
    *rest,
    window_slabs,
    slab_total,
    chunk,
    unroll,
):
    outs = rest[:window_slabs]
    matrix_ref, orbitals_ref, quad_ref, proj_ref, folded, acc = rest[window_slabs : window_slabs + 6]
    cell_ref, atom_ref, scale_ref, sems, small_sems = rest[window_slabs + 6 :]
    rows, parts, projs, nodes = folded.shape
    atoms = outs[0].shape[0]
    cells, orbs, _ = orbitals_ref.shape
    slab = lax.axis_index("cells")
    chunks = rows // chunk

    def columns(i):
        return pl.ds(i * nodes, nodes)

    load_quad = pltpu.make_async_copy(quad_hbm, quad_ref, sems.at[0])
    load_matrix = [
        pltpu.make_async_copy(
            matrix_hbm.at[:, columns(i)], matrix_ref.at[:, columns(i)], sems.at[1 + i]
        )
        for i in range(parts - 1)
    ]
    load_proj = [
        pltpu.make_async_copy(
            proj_hbm.at[pl.ds(c * chunk, chunk)],
            proj_ref.at[pl.ds(c * chunk, chunk)],
            sems.at[parts + c],
        )
        for c in range(chunks)
    ]
    load_orbitals = pltpu.make_async_copy(orbitals_hbm, orbitals_ref, sems.at[parts + chunks])
    load_small = [
        pltpu.make_async_copy(source, target, small_sems.at[k])
        for k, (source, target) in enumerate(
            ((cell_hbm, cell_ref), (atom_hbm, atom_ref), (scale_hbm, scale_ref))
        )
    ]
    load_quad.start()
    load_proj[0].start()
    for load in load_matrix:
        load.start()
    for load in load_proj[1:]:
        load.start()
    for load in load_small:
        load.start()
    acc[...] = jnp.zeros_like(acc)
    load_quad.wait()
    load_proj[0].wait()
    load_orbitals.start()

    for c in range(chunks):
        if c > 0:
            load_proj[c].wait()
        at = pl.ds(c * chunk, chunk)
        scaled = (proj_ref[at].astype(jnp.float32) * quad_ref[...][None]).astype(jnp.bfloat16)
        folded[at, 0] = scaled
        flat = scaled.reshape(chunk * projs, nodes)
        for i in range(parts - 1):
            if c == 0:
                load_matrix[i].wait()
            part = lax.dot_general(
                flat,
                matrix_ref[:, i * nodes : (i + 1) * nodes],
                CONTRACT_LAST,
                preferred_element_type=jnp.float32,
            )
            folded[at, i + 1] = part.astype(jnp.bfloat16).reshape(chunk, projs, nodes)
    load_orbitals.wait()
    for load in load_small:
        load.wait()

    def place(row):
        atom = atom_ref[row]
        owner = lax.div(jnp.maximum(atom, 0), atoms)
        relative = owner - slab + REACH
        relative = jnp.where(relative < 0, relative + slab_total, relative)
        relative = jnp.where(relative >= slab_total, relative - slab_total, relative)
        slot = (relative - owner) * atoms + atom
        return jnp.where(atom < 0, window_slabs * atoms, slot)

    def add_rows(step, carry):
        terms = []
        for j in range(unroll):
            row = step * unroll + j
            cell = cell_ref[row] - slab * cells
            term = lax.dot_general(
                folded[row].reshape(parts * projs, nodes),
                orbitals_ref[cell],
                CONTRACT_LAST,
                preferred_element_type=jnp.float32,
            )
            terms.append((place(row), scale_ref[cell], term))
        for slot, factor, term in terms:
            acc[slot, :projs] += term[:projs]
            acc[slot, projs:] += term[projs:] * factor
        return carry

    lax.fori_loop(0, rows // unroll, add_rows, 0)
    fold_by = LANES // orbs
    high = parts * projs // fold_by
    for window in range(window_slabs):
        for atom in range(atoms):
            whole = acc[window * atoms + atom]
            outs[window][atom] = jnp.concatenate(
                [whole[k * high : (k + 1) * high] for k in range(fold_by)], axis=1
            )


def window_sums(
    support_cell, support_atom, cell_scale, quad_weights, proj_values, gradient_matrix, orbitals, atoms, slab_total
):
    rows, projs, nodes = proj_values.shape
    cells, orbs, _ = orbitals.shape
    window_slabs = 2 * REACH + 1
    parts = 1 + gradient_matrix.shape[1] // nodes
    packed = (atoms, parts * projs * orbs // LANES, LANES)
    chunk = math.gcd(rows, 64)
    flops = 2 * rows * projs * nodes * (nodes * (parts - 1) + orbs * parts)
    results = pl.pallas_call(
        functools.partial(
            force_kernel,
            window_slabs=window_slabs,
            slab_total=slab_total,
            chunk=chunk,
            unroll=chunk,
        ),
        out_shape=[jax.ShapeDtypeStruct(packed, jnp.float32)] * window_slabs
        + [
            jax.ShapeDtypeStruct(gradient_matrix.shape, jnp.bfloat16),
            jax.ShapeDtypeStruct(orbitals.shape, jnp.bfloat16),
        ],
        in_specs=[HBM] * 7,
        out_specs=[VMEM] * (window_slabs + 2),
        compiler_params=pltpu.CompilerParams(vmem_limit_bytes=FORCE_MIB << 20),
        scratch_shapes=[
            pltpu.VMEM((1, nodes), jnp.float32),
            pltpu.VMEM(proj_values.shape, jnp.bfloat16),
            pltpu.VMEM((rows, parts, projs, nodes), jnp.bfloat16),
            pltpu.VMEM((window_slabs * atoms + 1, parts * projs, orbs), jnp.float32),
            pltpu.SMEM((rows,), jnp.int32),
            pltpu.SMEM((rows,), jnp.int32),
            pltpu.SMEM((cells,), jnp.float32),
            pltpu.SemaphoreType.DMA((parts + rows // chunk + 1,)),
            pltpu.SemaphoreType.DMA((3,)),
        ],
        cost_estimate=pl.CostEstimate(
            flops=flops, bytes_accessed=2 * orbitals.size + 2 * proj_values.size, transcendentals=0
        ),
        name="window_sums",
    )(
        *(
            pltpu.with_memory_space_constraint(operand, pltpu.HBM)
            for operand in (
                support_cell,
                support_atom,
                cell_scale,
                quad_weights.reshape(1, nodes),
                proj_values,
                gradient_matrix,
                orbitals,
            )
        )
    )
    return results[:window_slabs], results[window_slabs], results[window_slabs + 1]


def stress_kernel(
    occ_ref,
    quad_ref,
    scale_ref,
    matrix_ref,
    orbitals_ref,
    out_ref,
    even,
    odd,
    weight_ref,
    sums,
    *,
    share,
    block,
):
    orbs, nodes = weight_ref.shape
    cells = out_ref.shape[1]
    blocks = cells // block

    across = jnp.broadcast_to(occ_ref[...], (orbs, orbs))
    rows = lax.broadcasted_iota(jnp.int32, (orbs, orbs), 0)
    columns = lax.broadcasted_iota(jnp.int32, (orbs, orbs), 1)
    down = jnp.sum(jnp.where(rows == columns, across, 0.0), axis=1, keepdims=True)
    weight_ref[...] = down * quad_ref[...] * share

    def gradient_part(i, buffer, part):
        at = slice(part * nodes, (part + 1) * nodes)
        flat = orbitals_ref[pl.ds(pl.multiple_of(i * block, block), block)]
        buffer[:, at] = jnp.dot(
            flat.reshape(block * orbs, nodes), matrix_ref[:, at], preferred_element_type=jnp.float32
        )

    def reduce_cells(buffer, first, last, totals):
        for cell in range(first, last):
            acc = [None] * len(PAIRS)
            for group in range(orbs // SUBLANES):
                at = slice(group * SUBLANES, (group + 1) * SUBLANES)
                row = cell * orbs + group * SUBLANES
                weight = weight_ref[at, :]
                grad = [
                    buffer[row : row + SUBLANES, i * nodes : (i + 1) * nodes] for i in range(3)
                ]
                scaled = [weight * grad[i] for i in range(3)]
                for k, (a, b) in enumerate(PAIRS):
                    term = scaled[a] * grad[b]
                    acc[k] = term if acc[k] is None else acc[k] + term
            for k in range(len(PAIRS)):
                lanes = acc[k][:, :LANES]
                for c in range(1, nodes // LANES):
                    lanes = lanes + acc[k][:, c * LANES : (c + 1) * LANES]
                totals[k].append(jnp.sum(lanes, axis=0, keepdims=True))

    def store(i, totals):
        at = pl.ds(pl.multiple_of(i * block, block), block)
        for k in range(len(PAIRS)):
            sums[k, at, :] = jnp.concatenate(totals[k], axis=0)

    def both(i, full, empty):
        totals = [[] for _ in PAIRS]
        for part in range(3):
            reduce_cells(full, part * block // 3, (part + 1) * block // 3, totals)
            gradient_part(i + 1, empty, part)
        store(i, totals)

    for part in range(3):
        gradient_part(0, even, part)

    def pair(t, carry):
        both(2 * t, even, odd)
        both(2 * t + 1, odd, even)
        return carry

    lax.fori_loop(0, blocks // 2 - 1, pair, 0)
    both(blocks - 2, even, odd)
    totals = [[] for _ in PAIRS]
    reduce_cells(odd, 0, block, totals)
    store(blocks - 1, totals)

    whole = [jnp.sum(jnp.transpose(sums[k]), axis=0, keepdims=True) for k in range(len(PAIRS))]
    half = 0.5 * (whole[0] + whole[1] + whole[2])
    square = scale_ref[...] * scale_ref[...]
    for k in range(3):
        out_ref[k : k + 1, :] = (half - whole[k]) * square
    for k in range(3, 6):
        out_ref[k : k + 1, :] = -whole[k] * square


def stress_sums(occupations, quad_weights, cell_scale, gradient_matrix, orbitals, orbital_total):
    cells, orbs, nodes = orbitals.shape
    block = min(1024 // orbs, cells // 2)
    columns = gradient_matrix.shape[1]
    return pl.pallas_call(
        functools.partial(stress_kernel, share=1.0 / orbital_total, block=block),
        out_shape=jax.ShapeDtypeStruct((6, cells), jnp.float32),
        in_specs=[VMEM, VMEM, VMEM, VMEM, VMEM],
        out_specs=VMEM,
        compiler_params=pltpu.CompilerParams(vmem_limit_bytes=STRESS_MIB << 20),
        scratch_shapes=[
            pltpu.VMEM((block * orbs, columns), jnp.float32),
            pltpu.VMEM((block * orbs, columns), jnp.float32),
            pltpu.VMEM((orbs, nodes), jnp.float32),
            pltpu.VMEM((6, cells, LANES), jnp.float32),
        ],
        cost_estimate=pl.CostEstimate(
            flops=2 * orbitals.size * columns, bytes_accessed=2 * orbitals.size, transcendentals=0
        ),
        name="stress_sums",
    )(
        occupations.reshape(1, orbs),
        quad_weights.reshape(1, nodes),
        cell_scale.reshape(1, cells),
        gradient_matrix,
        orbitals,
    )


def local(
    orbitals,
    gradient_matrix,
    quad_weights,
    cell_scale,
    occupations,
    support_cell,
    support_atom,
    proj_values,
    proj_coupling,
):
    cells, orbital_count, node_count = orbitals.shape
    proj_count = proj_values.shape[1]
    atom_total = proj_coupling.shape[0]
    slab_total = lax.axis_size("cells")
    atom_share = atom_total // slab_total
    slab_index = lax.axis_index("cells")
    orbital_total = orbital_count * lax.axis_size("orb")

    parts, near_matrix, near_orbitals = window_sums(
        support_cell,
        support_atom,
        cell_scale,
        quad_weights,
        proj_values,
        gradient_matrix,
        orbitals,
        atom_share,
        slab_total,
    )
    owned = parts[REACH]
    for offset in range(-REACH, REACH + 1):
        if offset != 0:
            owned = owned + from_behind(parts[offset + REACH], "cells", offset)

    stress_part = stress_sums(
        occupations, quad_weights, cell_scale, near_matrix, near_orbitals, orbital_total
    )

    fold_by = LANES // orbital_count
    owned = jnp.concatenate(
        [owned[:, :, k * orbital_count : (k + 1) * orbital_count] for k in range(fold_by)], axis=1
    )
    owned = owned.reshape(atom_share, 4, proj_count, orbital_count)
    coupling = lax.dynamic_slice_in_dim(proj_coupling, slab_index * atom_share, atom_share, 0)
    weight_terms = coupling[:, :, None] * occupations[None, None, :]
    force_part = -2.0 * jnp.sum(owned[:, 1:] * (owned[:, 0] * weight_terms)[:, None], axis=(2, 3))
    force_part = jnp.pad(
        jnp.transpose(force_part), ((0, SUBLANES - 3), (0, cells - atom_share))
    )
    packed = jnp.concatenate([stress_part, jnp.zeros((2, cells), jnp.float32), force_part], axis=0)
    copies = [packed] + [from_behind(packed, "orb", by) for by in range(1, lax.axis_size("orb"))]
    total = functools.reduce(jnp.add, copies)
    return (total[:6], total[8:11, :atom_share])


def solution(mesh):
    return jax.shard_map(
        local,
        mesh=mesh,
        in_specs=(
            P("cells", "orb", None),
            P(),
            P(),
            P("cells"),
            P("orb"),
            P("cells"),
            P("cells"),
            P("cells", None, None),
            P(),
        ),
        out_specs=(P(None, "cells"), P(None, "cells")),
        check_vma=False,
    )
```

```python
import functools
import math

import jax
import jax.numpy as jnp
from jax import lax
from jax.experimental import pallas as pl
from jax.experimental.pallas import tpu as pltpu
from jax.sharding import PartitionSpec as P

REACH = 2
LANES = 128
SUBLANES = 8
PAIRS = ((0, 0), (1, 1), (2, 2), (0, 1), (0, 2), (1, 2))
CONTRACT_LAST = (((1,), (1,)), ((), ()))
FORCE_MIB, STRESS_MIB = 28, 30
SMEM = pl.BlockSpec(memory_space=pltpu.SMEM)
VMEM = pl.BlockSpec(memory_space=pltpu.VMEM)
HBM = pl.BlockSpec(memory_space=pltpu.HBM)


def from_behind(shard, axis, by):
    length = lax.axis_size(axis)
    return lax.ppermute(shard, axis, [(i, (i + by) % length) for i in range(length)])


def force_kernel(
    cell_hbm,
    atom_hbm,
    scale_hbm,
    quad_hbm,
    proj_hbm,
    matrix_hbm,
    orbitals_hbm,
    *rest,
    window_slabs,
    slab_total,
    chunk,
    unroll,
):
    outs = rest[:window_slabs]
    matrix_ref, orbitals_ref, quad_ref, proj_ref, folded, acc = rest[window_slabs : window_slabs + 6]
    cell_ref, atom_ref, scale_ref, sems, small_sems = rest[window_slabs + 6 :]
    rows, parts, projs, nodes = folded.shape
    atoms = outs[0].shape[0]
    cells, orbs, _ = orbitals_ref.shape
    slab = lax.axis_index("cells")
    chunks = rows // chunk

    def columns(i):
        return pl.ds(i * nodes, nodes)

    load_quad = pltpu.make_async_copy(quad_hbm, quad_ref, sems.at[0])
    load_matrix = [
        pltpu.make_async_copy(
            matrix_hbm.at[:, columns(i)], matrix_ref.at[:, columns(i)], sems.at[1 + i]
        )
        for i in range(parts - 1)
    ]
    load_proj = [
        pltpu.make_async_copy(
            proj_hbm.at[pl.ds(c * chunk, chunk)],
            proj_ref.at[pl.ds(c * chunk, chunk)],
            sems.at[parts + c],
        )
        for c in range(chunks)
    ]
    load_orbitals = pltpu.make_async_copy(orbitals_hbm, orbitals_ref, sems.at[parts + chunks])
    load_small = [
        pltpu.make_async_copy(source, target, small_sems.at[k])
        for k, (source, target) in enumerate(
            ((cell_hbm, cell_ref), (atom_hbm, atom_ref), (scale_hbm, scale_ref))
        )
    ]
    load_quad.start()
    load_proj[0].start()
    for load in load_matrix:
        load.start()
    for load in load_proj[1:]:
        load.start()
    for load in load_small:
        load.start()
    acc[...] = jnp.zeros_like(acc)
    load_quad.wait()
    load_proj[0].wait()
    load_orbitals.start()

    for c in range(chunks):
        if c > 0:
            load_proj[c].wait()
        at = pl.ds(c * chunk, chunk)
        scaled = (proj_ref[at].astype(jnp.float32) * quad_ref[...][None]).astype(jnp.bfloat16)
        folded[at, 0] = scaled
        flat = scaled.reshape(chunk * projs, nodes)
        for i in range(parts - 1):
            if c == 0:
                load_matrix[i].wait()
            part = lax.dot_general(
                flat,
                matrix_ref[:, i * nodes : (i + 1) * nodes],
                CONTRACT_LAST,
                preferred_element_type=jnp.float32,
            )
            folded[at, i + 1] = part.astype(jnp.bfloat16).reshape(chunk, projs, nodes)
    load_orbitals.wait()
    for load in load_small:
        load.wait()

    def place(row):
        atom = atom_ref[row]
        owner = lax.div(jnp.maximum(atom, 0), atoms)
        relative = owner - slab + REACH
        relative = jnp.where(relative < 0, relative + slab_total, relative)
        relative = jnp.where(relative >= slab_total, relative - slab_total, relative)
        slot = (relative - owner) * atoms + atom
        return jnp.where(atom < 0, window_slabs * atoms, slot)

    def add_rows(step, carry):
        terms = []
        for j in range(unroll):
            row = step * unroll + j
            cell = cell_ref[row] - slab * cells
            term = lax.dot_general(
                folded[row].reshape(parts * projs, nodes),
                orbitals_ref[cell],
                CONTRACT_LAST,
                preferred_element_type=jnp.float32,
            )
            terms.append((place(row), scale_ref[cell], term))
        for slot, factor, term in terms:
            acc[slot, :projs] += term[:projs]
            acc[slot, projs:] += term[projs:] * factor
        return carry

    lax.fori_loop(0, rows // unroll, add_rows, 0)
    fold_by = LANES // orbs
    high = parts * projs // fold_by
    for window in range(window_slabs):
        for atom in range(atoms):
            whole = acc[window * atoms + atom]
            outs[window][atom] = jnp.concatenate(
                [whole[k * high : (k + 1) * high] for k in range(fold_by)], axis=1
            )


def window_sums(
    support_cell, support_atom, cell_scale, quad_weights, proj_values, gradient_matrix, orbitals, atoms, slab_total
):
    rows, projs, nodes = proj_values.shape
    cells, orbs, _ = orbitals.shape
    window_slabs = 2 * REACH + 1
    parts = 1 + gradient_matrix.shape[1] // nodes
    packed = (atoms, parts * projs * orbs // LANES, LANES)
    chunk = math.gcd(rows, 64)
    flops = 2 * rows * projs * nodes * (nodes * (parts - 1) + orbs * parts)
    results = pl.pallas_call(
        functools.partial(
            force_kernel,
            window_slabs=window_slabs,
            slab_total=slab_total,
            chunk=chunk,
            unroll=chunk,
        ),
        out_shape=[jax.ShapeDtypeStruct(packed, jnp.float32)] * window_slabs
        + [
            jax.ShapeDtypeStruct(gradient_matrix.shape, jnp.bfloat16),
            jax.ShapeDtypeStruct(orbitals.shape, jnp.bfloat16),
        ],
        in_specs=[HBM] * 7,
        out_specs=[VMEM] * (window_slabs + 2),
        compiler_params=pltpu.CompilerParams(vmem_limit_bytes=FORCE_MIB << 20),
        scratch_shapes=[
            pltpu.VMEM((1, nodes), jnp.float32),
            pltpu.VMEM(proj_values.shape, jnp.bfloat16),
            pltpu.VMEM((rows, parts, projs, nodes), jnp.bfloat16),
            pltpu.VMEM((window_slabs * atoms + 1, parts * projs, orbs), jnp.float32),
            pltpu.SMEM((rows,), jnp.int32),
            pltpu.SMEM((rows,), jnp.int32),
            pltpu.SMEM((cells,), jnp.float32),
            pltpu.SemaphoreType.DMA((parts + rows // chunk + 1,)),
            pltpu.SemaphoreType.DMA((3,)),
        ],
        cost_estimate=pl.CostEstimate(
            flops=flops, bytes_accessed=2 * orbitals.size + 2 * proj_values.size, transcendentals=0
        ),
        name="window_sums",
    )(
        *(
            pltpu.with_memory_space_constraint(operand, pltpu.HBM)
            for operand in (
                support_cell,
                support_atom,
                cell_scale,
                quad_weights.reshape(1, nodes),
                proj_values,
                gradient_matrix,
                orbitals,
            )
        )
    )
    return results[:window_slabs], results[window_slabs], results[window_slabs + 1]


def stress_kernel(
    occ_ref,
    quad_ref,
    scale_ref,
    matrix_ref,
    orbitals_ref,
    out_ref,
    even,
    odd,
    weight_ref,
    sums,
    *,
    share,
    block,
):
    orbs, nodes = weight_ref.shape
    cells = out_ref.shape[1]
    blocks = cells // block

    across = jnp.broadcast_to(occ_ref[...], (orbs, orbs))
    rows = lax.broadcasted_iota(jnp.int32, (orbs, orbs), 0)
    columns = lax.broadcasted_iota(jnp.int32, (orbs, orbs), 1)
    down = jnp.sum(jnp.where(rows == columns, across, 0.0), axis=1, keepdims=True)
    weight_ref[...] = down * quad_ref[...] * share

    def gradient_part(i, buffer, part):
        at = slice(part * nodes, (part + 1) * nodes)
        flat = orbitals_ref[pl.ds(pl.multiple_of(i * block, block), block)]
        buffer[:, at] = jnp.dot(
            flat.reshape(block * orbs, nodes), matrix_ref[:, at], preferred_element_type=jnp.float32
        )

    def reduce_cells(buffer, first, last, totals):
        for cell in range(first, last):
            acc = [None] * len(PAIRS)
            for group in range(orbs // SUBLANES):
                at = slice(group * SUBLANES, (group + 1) * SUBLANES)
                row = cell * orbs + group * SUBLANES
                weight = weight_ref[at, :]
                grad = [
                    buffer[row : row + SUBLANES, i * nodes : (i + 1) * nodes] for i in range(3)
                ]
                scaled = [weight * grad[i] for i in range(3)]
                for k, (a, b) in enumerate(PAIRS):
                    term = scaled[a] * grad[b]
                    acc[k] = term if acc[k] is None else acc[k] + term
            for k in range(len(PAIRS)):
                lanes = acc[k][:, :LANES]
                for c in range(1, nodes // LANES):
                    lanes = lanes + acc[k][:, c * LANES : (c + 1) * LANES]
                totals[k].append(jnp.sum(lanes, axis=0, keepdims=True))

    def store(i, totals):
        at = pl.ds(pl.multiple_of(i * block, block), block)
        for k in range(len(PAIRS)):
            sums[k, at, :] = jnp.concatenate(totals[k], axis=0)

    def both(i, full, empty):
        totals = [[] for _ in PAIRS]
        for part in range(3):
            reduce_cells(full, part * block // 3, (part + 1) * block // 3, totals)
            gradient_part(i + 1, empty, part)
        store(i, totals)

    for part in range(3):
        gradient_part(0, even, part)

    def pair(t, carry):
        both(2 * t, even, odd)
        both(2 * t + 1, odd, even)
        return carry

    lax.fori_loop(0, blocks // 2 - 1, pair, 0)
    both(blocks - 2, even, odd)
    totals = [[] for _ in PAIRS]
    reduce_cells(odd, 0, block, totals)
    store(blocks - 1, totals)

    whole = [jnp.sum(jnp.transpose(sums[k]), axis=0, keepdims=True) for k in range(len(PAIRS))]
    half = 0.5 * (whole[0] + whole[1] + whole[2])
    square = scale_ref[...] * scale_ref[...]
    for k in range(3):
        out_ref[k : k + 1, :] = (half - whole[k]) * square
    for k in range(3, 6):
        out_ref[k : k + 1, :] = -whole[k] * square


def stress_sums(occupations, quad_weights, cell_scale, gradient_matrix, orbitals, orbital_total):
    cells, orbs, nodes = orbitals.shape
    block = min(1024 // orbs, cells // 2)
    columns = gradient_matrix.shape[1]
    return pl.pallas_call(
        functools.partial(stress_kernel, share=1.0 / orbital_total, block=block),
        out_shape=jax.ShapeDtypeStruct((6, cells), jnp.float32),
        in_specs=[VMEM, VMEM, VMEM, VMEM, VMEM],
        out_specs=VMEM,
        compiler_params=pltpu.CompilerParams(vmem_limit_bytes=STRESS_MIB << 20),
        scratch_shapes=[
            pltpu.VMEM((block * orbs, columns), jnp.float32),
            pltpu.VMEM((block * orbs, columns), jnp.float32),
            pltpu.VMEM((orbs, nodes), jnp.float32),
            pltpu.VMEM((6, cells, LANES), jnp.float32),
        ],
        cost_estimate=pl.CostEstimate(
            flops=2 * orbitals.size * columns, bytes_accessed=2 * orbitals.size, transcendentals=0
        ),
        name="stress_sums",
    )(
        occupations.reshape(1, orbs),
        quad_weights.reshape(1, nodes),
        cell_scale.reshape(1, cells),
        gradient_matrix,
        orbitals,
    )


def combine_kernel(*refs, windows):
    parts = refs[:windows]
    coupling_ref, occ_ref, stress_ref, out_ref = refs[windows:]
    atoms, high, _ = parts[0].shape
    orbs = occ_ref.shape[1]
    projs = coupling_ref.shape[1]
    components = high * LANES // orbs // projs - 1
    slab = lax.axis_index("cells")
    share = coupling_ref[pl.ds(pl.multiple_of(slab * atoms, atoms), atoms), :]
    down = jnp.transpose(share)
    rows = [[] for _ in range(components)]
    for atom in range(atoms):
        total = parts[0][atom]
        for part in parts[1:]:
            total = total + part[atom]
        whole = jnp.concatenate(
            [total[:, k * orbs : (k + 1) * orbs] for k in range(LANES // orbs)], axis=0
        )
        margin = whole[:projs] * (down[:, atom : atom + 1] * occ_ref[...])
        for i in range(components):
            deriv = whole[(i + 1) * projs : (i + 2) * projs]
            rows[i].append(jnp.sum(margin * deriv, axis=0, keepdims=True))
    lane = lax.broadcasted_iota(jnp.int32, (atoms, LANES), 1)
    line = lax.broadcasted_iota(jnp.int32, (atoms, LANES), 0)
    out_ref[...] = jnp.zeros_like(out_ref)
    out_ref[: stress_ref.shape[0], :] = stress_ref[...]
    for i in range(components):
        force = -2.0 * jnp.sum(jnp.concatenate(rows[i], axis=0), axis=1, keepdims=True)
        out_ref[SUBLANES + i : SUBLANES + i + 1, :LANES] = jnp.sum(
            jnp.where(lane == line, force, 0.0), axis=0, keepdims=True
        )


def combine(parts, proj_coupling, occupations, stress_part, slab_total):
    return pl.pallas_call(
        functools.partial(combine_kernel, windows=len(parts)),
        out_shape=jax.ShapeDtypeStruct((2 * SUBLANES, stress_part.shape[1]), jnp.float32),
        in_specs=[VMEM] * (len(parts) + 3),
        out_specs=VMEM,
        compiler_params=pltpu.CompilerParams(vmem_limit_bytes=8 << 20),
        name="combine",
    )(*parts, proj_coupling, occupations.reshape(1, -1), stress_part)


def add_kernel(*refs):
    stress_ref, force_ref = refs[-2:]
    total = refs[0][...]
    for ref in refs[1:-2]:
        total = total + ref[...]
    stress_ref[...] = total[: stress_ref.shape[0]]
    force_ref[...] = total[SUBLANES : SUBLANES + force_ref.shape[0], : force_ref.shape[1]]


def add_up(copies, atoms):
    return pl.pallas_call(
        add_kernel,
        out_shape=(
            jax.ShapeDtypeStruct((len(PAIRS), copies[0].shape[1]), jnp.float32),
            jax.ShapeDtypeStruct((3, atoms), jnp.float32),
        ),
        in_specs=[VMEM] * len(copies),
        out_specs=(VMEM, VMEM),
        compiler_params=pltpu.CompilerParams(vmem_limit_bytes=8 << 20),
        name="add_up",
    )(*copies)


def local(
    orbitals,
    gradient_matrix,
    quad_weights,
    cell_scale,
    occupations,
    support_cell,
    support_atom,
    proj_values,
    proj_coupling,
):
    cells, orbital_count, node_count = orbitals.shape
    atom_total = proj_coupling.shape[0]
    slab_total = lax.axis_size("cells")
    atom_share = atom_total // slab_total
    orbital_total = orbital_count * lax.axis_size("orb")

    parts, near_matrix, near_orbitals = window_sums(
        support_cell,
        support_atom,
        cell_scale,
        quad_weights,
        proj_values,
        gradient_matrix,
        orbitals,
        atom_share,
        slab_total,
    )
    received = [
        from_behind(parts[offset + REACH], "cells", offset) for offset in (2, 1, -1, -2)
    ]

    stress_part = stress_sums(
        occupations, quad_weights, cell_scale, near_matrix, near_orbitals, orbital_total
    )

    packed = combine(
        [parts[REACH]] + received, proj_coupling, occupations, stress_part, slab_total
    )
    size = lax.axis_size("orb")
    copies = [packed] + [
        lax.ppermute(packed, "orb", [(i, i ^ by) for i in range(size)]) for by in range(size - 1, 0, -1)
    ]
    return add_up(copies, atom_share)


def solution(mesh):
    return jax.shard_map(
        local,
        mesh=mesh,
        in_specs=(
            P("cells", "orb", None),
            P(),
            P(),
            P("cells"),
            P("orb"),
            P("cells"),
            P("cells"),
            P("cells", None, None),
            P(),
        ),
        out_specs=(P(None, "cells"), P(None, "cells")),
        check_vma=False,
    )
```

```python
import functools
import math

import jax
import jax.numpy as jnp
from jax import lax
from jax.experimental import pallas as pl
from jax.experimental.pallas import tpu as pltpu
from jax.sharding import PartitionSpec as P

REACH = 2
LANES = 128
SUBLANES = 8
PAIRS = ((0, 0), (1, 1), (2, 2), (0, 1), (0, 2), (1, 2))
CONTRACT_LAST = (((1,), (1,)), ((), ()))
FORCE_MIB, STRESS_MIB = 28, 30
SMEM = pl.BlockSpec(memory_space=pltpu.SMEM)
VMEM = pl.BlockSpec(memory_space=pltpu.VMEM)
HBM = pl.BlockSpec(memory_space=pltpu.HBM)


def from_behind(shard, axis, by):
    length = lax.axis_size(axis)
    return lax.ppermute(shard, axis, [(i, (i + by) % length) for i in range(length)])


def force_kernel(
    cell_hbm,
    atom_hbm,
    scale_hbm,
    quad_hbm,
    proj_hbm,
    matrix_hbm,
    orbitals_hbm,
    *rest,
    window_slabs,
    slab_total,
    chunk,
    unroll,
):
    outs = rest[:window_slabs]
    matrix_ref, orbitals_ref, quad_ref, proj_ref, folded, acc = rest[window_slabs : window_slabs + 6]
    cell_ref, atom_ref, scale_ref, sems, small_sems = rest[window_slabs + 6 :]
    rows, parts, projs, nodes = folded.shape
    atoms = outs[0].shape[0]
    cells, orbs, _ = orbitals_ref.shape
    slab = lax.axis_index("cells")
    chunks = rows // chunk

    def columns(i):
        return pl.ds(i * nodes, nodes)

    load_quad = pltpu.make_async_copy(quad_hbm, quad_ref, sems.at[0])
    load_matrix = [
        pltpu.make_async_copy(
            matrix_hbm.at[:, columns(i)], matrix_ref.at[:, columns(i)], sems.at[1 + i]
        )
        for i in range(parts - 1)
    ]
    load_proj = [
        pltpu.make_async_copy(
            proj_hbm.at[pl.ds(c * chunk, chunk)],
            proj_ref.at[pl.ds(c * chunk, chunk)],
            sems.at[parts + c],
        )
        for c in range(chunks)
    ]
    load_orbitals = pltpu.make_async_copy(orbitals_hbm, orbitals_ref, sems.at[parts + chunks])
    load_small = [
        pltpu.make_async_copy(source, target, small_sems.at[k])
        for k, (source, target) in enumerate(
            ((cell_hbm, cell_ref), (atom_hbm, atom_ref), (scale_hbm, scale_ref))
        )
    ]
    load_quad.start()
    load_proj[0].start()
    for load in load_matrix:
        load.start()
    for load in load_proj[1:]:
        load.start()
    for load in load_small:
        load.start()
    acc[...] = jnp.zeros_like(acc)
    load_quad.wait()
    load_proj[0].wait()
    load_orbitals.start()

    for c in range(chunks):
        if c > 0:
            load_proj[c].wait()
        at = pl.ds(c * chunk, chunk)
        scaled = (proj_ref[at].astype(jnp.float32) * quad_ref[...][None]).astype(jnp.bfloat16)
        folded[at, 0] = scaled
        flat = scaled.reshape(chunk * projs, nodes)
        for i in range(parts - 1):
            if c == 0:
                load_matrix[i].wait()
            part = lax.dot_general(
                flat,
                matrix_ref[:, i * nodes : (i + 1) * nodes],
                CONTRACT_LAST,
                preferred_element_type=jnp.float32,
            )
            folded[at, i + 1] = part.astype(jnp.bfloat16).reshape(chunk, projs, nodes)
    load_orbitals.wait()
    for load in load_small:
        load.wait()

    def place(row):
        atom = atom_ref[row]
        owner = lax.div(jnp.maximum(atom, 0), atoms)
        relative = owner - slab + REACH
        relative = jnp.where(relative < 0, relative + slab_total, relative)
        relative = jnp.where(relative >= slab_total, relative - slab_total, relative)
        slot = (relative - owner) * atoms + atom
        return jnp.where(atom < 0, window_slabs * atoms, slot)

    def add_rows(step, carry):
        terms = []
        for j in range(unroll):
            row = step * unroll + j
            cell = cell_ref[row] - slab * cells
            term = lax.dot_general(
                folded[row].reshape(parts * projs, nodes),
                orbitals_ref[cell],
                CONTRACT_LAST,
                preferred_element_type=jnp.float32,
            )
            terms.append((place(row), scale_ref[cell], term))
        for slot, factor, term in terms:
            acc[slot, :projs] += term[:projs]
            acc[slot, projs:] += term[projs:] * factor
        return carry

    lax.fori_loop(0, rows // unroll, add_rows, 0)
    fold_by = LANES // orbs
    high = parts * projs // fold_by
    for window in range(window_slabs):
        for atom in range(atoms):
            whole = acc[window * atoms + atom]
            outs[window][atom] = jnp.concatenate(
                [whole[k * high : (k + 1) * high] for k in range(fold_by)], axis=1
            )


def window_sums(
    support_cell, support_atom, cell_scale, quad_weights, proj_values, gradient_matrix, orbitals, atoms, slab_total
):
    rows, projs, nodes = proj_values.shape
    cells, orbs, _ = orbitals.shape
    window_slabs = 2 * REACH + 1
    parts = 1 + gradient_matrix.shape[1] // nodes
    packed = (atoms, parts * projs * orbs // LANES, LANES)
    chunk = math.gcd(rows, 64)
    flops = 2 * rows * projs * nodes * (nodes * (parts - 1) + orbs * parts)
    results = pl.pallas_call(
        functools.partial(
            force_kernel,
            window_slabs=window_slabs,
            slab_total=slab_total,
            chunk=chunk,
            unroll=chunk,
        ),
        out_shape=[jax.ShapeDtypeStruct(packed, jnp.float32)] * window_slabs
        + [
            jax.ShapeDtypeStruct(gradient_matrix.shape, jnp.bfloat16),
            jax.ShapeDtypeStruct(orbitals.shape, jnp.bfloat16),
        ],
        in_specs=[HBM] * 7,
        out_specs=[VMEM] * (window_slabs + 2),
        compiler_params=pltpu.CompilerParams(vmem_limit_bytes=FORCE_MIB << 20),
        scratch_shapes=[
            pltpu.VMEM((1, nodes), jnp.float32),
            pltpu.VMEM(proj_values.shape, jnp.bfloat16),
            pltpu.VMEM((rows, parts, projs, nodes), jnp.bfloat16),
            pltpu.VMEM((window_slabs * atoms + 1, parts * projs, orbs), jnp.float32),
            pltpu.SMEM((rows,), jnp.int32),
            pltpu.SMEM((rows,), jnp.int32),
            pltpu.SMEM((cells,), jnp.float32),
            pltpu.SemaphoreType.DMA((parts + rows // chunk + 1,)),
            pltpu.SemaphoreType.DMA((3,)),
        ],
        cost_estimate=pl.CostEstimate(
            flops=flops, bytes_accessed=2 * orbitals.size + 2 * proj_values.size, transcendentals=0
        ),
        name="window_sums",
    )(
        *(
            pltpu.with_memory_space_constraint(operand, pltpu.HBM)
            for operand in (
                support_cell,
                support_atom,
                cell_scale,
                quad_weights.reshape(1, nodes),
                proj_values,
                gradient_matrix,
                orbitals,
            )
        )
    )
    return results[:window_slabs], results[window_slabs], results[window_slabs + 1]


def stress_kernel(
    occ_ref,
    quad_ref,
    scale_ref,
    matrix_ref,
    orbitals_ref,
    out_ref,
    even,
    odd,
    weight_ref,
    sums,
    *,
    share,
    block,
):
    orbs, nodes = weight_ref.shape
    cells = out_ref.shape[1]
    blocks = cells // block

    across = jnp.broadcast_to(occ_ref[...], (orbs, orbs))
    rows = lax.broadcasted_iota(jnp.int32, (orbs, orbs), 0)
    columns = lax.broadcasted_iota(jnp.int32, (orbs, orbs), 1)
    down = jnp.sum(jnp.where(rows == columns, across, 0.0), axis=1, keepdims=True)
    weight_ref[...] = down * quad_ref[...] * share

    def gradient_part(i, buffer, part, first=0, last=block):
        at = slice(part * nodes, (part + 1) * nodes)
        flat = orbitals_ref[pl.ds(i * block + first, last - first)]
        buffer[first * orbs : last * orbs, at] = jnp.dot(
            flat.reshape((last - first) * orbs, nodes),
            matrix_ref[:, at],
            preferred_element_type=jnp.float32,
        )

    def reduce_cells(buffer, first, last, totals):
        for cell in range(first, last):
            acc = [None] * len(PAIRS)
            for group in range(orbs // SUBLANES):
                at = slice(group * SUBLANES, (group + 1) * SUBLANES)
                row = cell * orbs + group * SUBLANES
                weight = weight_ref[at, :]
                grad = [
                    buffer[row : row + SUBLANES, i * nodes : (i + 1) * nodes] for i in range(3)
                ]
                scaled = [weight * grad[i] for i in range(3)]
                for k, (a, b) in enumerate(PAIRS):
                    term = scaled[a] * grad[b]
                    acc[k] = term if acc[k] is None else acc[k] + term
            for k in range(len(PAIRS)):
                lanes = acc[k][:, :LANES]
                for c in range(1, nodes // LANES):
                    lanes = lanes + acc[k][:, c * LANES : (c + 1) * LANES]
                totals[k].append(jnp.sum(lanes, axis=0, keepdims=True))

    def store(i, totals):
        at = pl.ds(pl.multiple_of(i * block, block), block)
        for k in range(len(PAIRS)):
            sums[k, at, :] = jnp.concatenate(totals[k], axis=0)

    def both(i, full, empty):
        totals = [[] for _ in PAIRS]
        for part in range(3):
            reduce_cells(full, part * block // 3, (part + 1) * block // 3, totals)
            gradient_part(i + 1, empty, part)
        store(i, totals)

    for part in range(3):
        gradient_part(0, even, part)

    def pair(t, carry):
        both(2 * t, even, odd)
        both(2 * t + 1, odd, even)
        return carry

    lax.fori_loop(0, blocks // 2 - 1, pair, 0)
    middle = block // 2
    before = [[] for _ in PAIRS]
    totals = [[] for _ in PAIRS]
    for part in range(3):
        reduce_cells(even, part * block // 3, (part + 1) * block // 3, before)
        gradient_part(blocks - 1, odd, part, 0, middle)
    store(blocks - 2, before)
    for part in range(3):
        reduce_cells(odd, part * middle // 3, (part + 1) * middle // 3, totals)
        gradient_part(blocks - 1, odd, part, middle, block)
    reduce_cells(odd, middle, block, totals)
    store(blocks - 1, totals)

    whole = [jnp.sum(jnp.transpose(sums[k]), axis=0, keepdims=True) for k in range(len(PAIRS))]
    half = 0.5 * (whole[0] + whole[1] + whole[2])
    square = scale_ref[...] * scale_ref[...]
    for k in range(3):
        out_ref[k : k + 1, :] = (half - whole[k]) * square
    for k in range(3, 6):
        out_ref[k : k + 1, :] = -whole[k] * square


def stress_sums(occupations, quad_weights, cell_scale, gradient_matrix, orbitals, orbital_total):
    cells, orbs, nodes = orbitals.shape
    block = min(1024 // orbs, cells // 2)
    columns = gradient_matrix.shape[1]
    return pl.pallas_call(
        functools.partial(stress_kernel, share=1.0 / orbital_total, block=block),
        out_shape=jax.ShapeDtypeStruct((6, cells), jnp.float32),
        in_specs=[VMEM, VMEM, VMEM, VMEM, VMEM],
        out_specs=VMEM,
        compiler_params=pltpu.CompilerParams(vmem_limit_bytes=STRESS_MIB << 20),
        scratch_shapes=[
            pltpu.VMEM((block * orbs, columns), jnp.float32),
            pltpu.VMEM((block * orbs, columns), jnp.float32),
            pltpu.VMEM((orbs, nodes), jnp.float32),
            pltpu.VMEM((6, cells, LANES), jnp.float32),
        ],
        cost_estimate=pl.CostEstimate(
            flops=2 * orbitals.size * columns, bytes_accessed=2 * orbitals.size, transcendentals=0
        ),
        name="stress_sums",
    )(
        occupations.reshape(1, orbs),
        quad_weights.reshape(1, nodes),
        cell_scale.reshape(1, cells),
        gradient_matrix,
        orbitals,
    )


def combine_kernel(*refs, windows):
    parts = refs[:windows]
    coupling_ref, occ_ref, stress_ref, out_ref = refs[windows:]
    atoms, high, _ = parts[0].shape
    orbs = occ_ref.shape[1]
    projs = coupling_ref.shape[1]
    components = high * LANES // orbs // projs - 1
    slab = lax.axis_index("cells")
    share = coupling_ref[pl.ds(pl.multiple_of(slab * atoms, atoms), atoms), :]
    down = jnp.transpose(share)
    rows = [[] for _ in range(components)]
    for atom in range(atoms):
        total = parts[0][atom]
        for part in parts[1:]:
            total = total + part[atom]
        whole = jnp.concatenate(
            [total[:, k * orbs : (k + 1) * orbs] for k in range(LANES // orbs)], axis=0
        )
        margin = whole[:projs] * (down[:, atom : atom + 1] * occ_ref[...])
        for i in range(components):
            deriv = whole[(i + 1) * projs : (i + 2) * projs]
            rows[i].append(jnp.sum(margin * deriv, axis=0, keepdims=True))
    lane = lax.broadcasted_iota(jnp.int32, (atoms, LANES), 1)
    line = lax.broadcasted_iota(jnp.int32, (atoms, LANES), 0)
    out_ref[...] = jnp.zeros_like(out_ref)
    out_ref[: stress_ref.shape[0], :] = stress_ref[...]
    for i in range(components):
        force = -2.0 * jnp.sum(jnp.concatenate(rows[i], axis=0), axis=1, keepdims=True)
        out_ref[SUBLANES + i : SUBLANES + i + 1, :LANES] = jnp.sum(
            jnp.where(lane == line, force, 0.0), axis=0, keepdims=True
        )


def combine(parts, proj_coupling, occupations, stress_part, slab_total):
    return pl.pallas_call(
        functools.partial(combine_kernel, windows=len(parts)),
        out_shape=jax.ShapeDtypeStruct((2 * SUBLANES, stress_part.shape[1]), jnp.float32),
        in_specs=[VMEM] * (len(parts) + 3),
        out_specs=VMEM,
        compiler_params=pltpu.CompilerParams(vmem_limit_bytes=8 << 20),
        name="combine",
    )(*parts, proj_coupling, occupations.reshape(1, -1), stress_part)


def add_kernel(*refs):
    stress_ref, force_ref = refs[-2:]
    total = refs[0][...]
    for ref in refs[1:-2]:
        total = total + ref[...]
    stress_ref[...] = total[: stress_ref.shape[0]]
    force_ref[...] = total[SUBLANES : SUBLANES + force_ref.shape[0], : force_ref.shape[1]]


def add_up(copies, atoms):
    return pl.pallas_call(
        add_kernel,
        out_shape=(
            jax.ShapeDtypeStruct((len(PAIRS), copies[0].shape[1]), jnp.float32),
            jax.ShapeDtypeStruct((3, atoms), jnp.float32),
        ),
        in_specs=[VMEM] * len(copies),
        out_specs=(VMEM, VMEM),
        compiler_params=pltpu.CompilerParams(vmem_limit_bytes=8 << 20),
        name="add_up",
    )(*copies)


def local(
    orbitals,
    gradient_matrix,
    quad_weights,
    cell_scale,
    occupations,
    support_cell,
    support_atom,
    proj_values,
    proj_coupling,
):
    cells, orbital_count, node_count = orbitals.shape
    atom_total = proj_coupling.shape[0]
    slab_total = lax.axis_size("cells")
    atom_share = atom_total // slab_total
    orbital_total = orbital_count * lax.axis_size("orb")

    parts, near_matrix, near_orbitals = window_sums(
        support_cell,
        support_atom,
        cell_scale,
        quad_weights,
        proj_values,
        gradient_matrix,
        orbitals,
        atom_share,
        slab_total,
    )
    received = [
        from_behind(parts[offset + REACH], "cells", offset) for offset in (2, 1, -1, -2)
    ]

    stress_part = stress_sums(
        occupations, quad_weights, cell_scale, near_matrix, near_orbitals, orbital_total
    )

    packed = combine(
        [parts[REACH]] + received, proj_coupling, occupations, stress_part, slab_total
    )
    size = lax.axis_size("orb")
    copies = [packed] + [
        lax.ppermute(packed, "orb", [(i, i ^ by) for i in range(size)]) for by in range(size - 1, 0, -1)
    ]
    return add_up(copies, atom_share)


def solution(mesh):
    return jax.shard_map(
        local,
        mesh=mesh,
        in_specs=(
            P("cells", "orb", None),
            P(),
            P(),
            P("cells"),
            P("orb"),
            P("cells"),
            P("cells"),
            P("cells", None, None),
            P(),
        ),
        out_specs=(P(None, "cells"), P(None, "cells")),
        check_vma=False,
    )
```

```python
import functools
import math

import jax
import jax.numpy as jnp
from jax import lax
from jax.experimental import pallas as pl
from jax.experimental.pallas import tpu as pltpu
from jax.sharding import PartitionSpec as P

REACH = 2
LANES = 128
SUBLANES = 8
PAIRS = ((0, 0), (1, 1), (2, 2), (0, 1), (0, 2), (1, 2))
CONTRACT_LAST = (((1,), (1,)), ((), ()))
FORCE_MIB, STRESS_MIB = 28, 30
SMEM = pl.BlockSpec(memory_space=pltpu.SMEM)
VMEM = pl.BlockSpec(memory_space=pltpu.VMEM)
HBM = pl.BlockSpec(memory_space=pltpu.HBM)


def from_behind(shard, axis, by):
    length = lax.axis_size(axis)
    return lax.ppermute(shard, axis, [(i, (i + by) % length) for i in range(length)])


def force_kernel(
    cell_hbm,
    atom_hbm,
    scale_hbm,
    quad_hbm,
    proj_hbm,
    matrix_hbm,
    orbitals_hbm,
    *rest,
    window_slabs,
    slab_total,
    chunk,
    unroll,
):
    outs = rest[:window_slabs]
    matrix_ref, orbitals_ref, quad_ref, proj_ref, folded, acc = rest[window_slabs : window_slabs + 6]
    cell_ref, atom_ref, scale_ref, sems, small_sems = rest[window_slabs + 6 :]
    rows, parts, projs, nodes = folded.shape
    atoms = outs[0].shape[0]
    cells, orbs, _ = orbitals_ref.shape
    slab = lax.axis_index("cells")
    chunks = rows // chunk

    def columns(i):
        return pl.ds(i * nodes, nodes)

    load_quad = pltpu.make_async_copy(quad_hbm, quad_ref, sems.at[0])
    load_matrix = [
        pltpu.make_async_copy(
            matrix_hbm.at[:, columns(i)], matrix_ref.at[:, columns(i)], sems.at[1 + i]
        )
        for i in range(parts - 1)
    ]
    load_proj = [
        pltpu.make_async_copy(
            proj_hbm.at[pl.ds(c * chunk, chunk)],
            proj_ref.at[pl.ds(c * chunk, chunk)],
            sems.at[parts + c],
        )
        for c in range(chunks)
    ]
    load_orbitals = pltpu.make_async_copy(orbitals_hbm, orbitals_ref, sems.at[parts + chunks])
    load_small = [
        pltpu.make_async_copy(source, target, small_sems.at[k])
        for k, (source, target) in enumerate(
            ((cell_hbm, cell_ref), (atom_hbm, atom_ref), (scale_hbm, scale_ref))
        )
    ]
    load_quad.start()
    load_proj[0].start()
    for load in load_matrix:
        load.start()
    for load in load_proj[1:]:
        load.start()
    for load in load_small:
        load.start()
    acc[...] = jnp.zeros_like(acc)
    load_quad.wait()
    load_proj[0].wait()
    for load in load_matrix:
        load.wait()
    load_orbitals.start()

    for c in range(chunks):
        if c > 0:
            load_proj[c].wait()
        at = pl.ds(c * chunk, chunk)
        scaled = (proj_ref[at].astype(jnp.float32) * quad_ref[...][None]).astype(jnp.bfloat16)
        folded[at, 0] = scaled
        flat = scaled.reshape(chunk * projs, nodes)
        for i in range(parts - 1):
            part = lax.dot_general(
                flat,
                matrix_ref[:, i * nodes : (i + 1) * nodes],
                CONTRACT_LAST,
                preferred_element_type=jnp.float32,
            )
            folded[at, i + 1] = part.astype(jnp.bfloat16).reshape(chunk, projs, nodes)
    load_orbitals.wait()
    for load in load_small:
        load.wait()

    def place(row):
        atom = atom_ref[row]
        owner = lax.div(jnp.maximum(atom, 0), atoms)
        relative = owner - slab + REACH
        relative = jnp.where(relative < 0, relative + slab_total, relative)
        relative = jnp.where(relative >= slab_total, relative - slab_total, relative)
        slot = (relative - owner) * atoms + atom
        return jnp.where(atom < 0, window_slabs * atoms, slot)

    def add_rows(step, carry):
        terms = []
        for j in range(unroll):
            row = step * unroll + j
            cell = cell_ref[row] - slab * cells
            term = lax.dot_general(
                folded[row].reshape(parts * projs, nodes),
                orbitals_ref[cell],
                CONTRACT_LAST,
                preferred_element_type=jnp.float32,
            )
            terms.append((place(row), scale_ref[cell], term))
        for slot, factor, term in terms:
            acc[slot, :projs] += term[:projs]
            acc[slot, projs:] += term[projs:] * factor
        return carry

    lax.fori_loop(0, rows // unroll, add_rows, 0)
    fold_by = LANES // orbs
    high = parts * projs // fold_by
    for window in range(window_slabs):
        for atom in range(atoms):
            whole = acc[window * atoms + atom]
            outs[window][atom] = jnp.concatenate(
                [whole[k * high : (k + 1) * high] for k in range(fold_by)], axis=1
            )


def window_sums(
    support_cell, support_atom, cell_scale, quad_weights, proj_values, gradient_matrix, orbitals, atoms, slab_total
):
    rows, projs, nodes = proj_values.shape
    cells, orbs, _ = orbitals.shape
    window_slabs = 2 * REACH + 1
    parts = 1 + gradient_matrix.shape[1] // nodes
    packed = (atoms, parts * projs * orbs // LANES, LANES)
    chunk = math.gcd(rows, 64)
    flops = 2 * rows * projs * nodes * (nodes * (parts - 1) + orbs * parts)
    results = pl.pallas_call(
        functools.partial(
            force_kernel,
            window_slabs=window_slabs,
            slab_total=slab_total,
            chunk=chunk,
            unroll=chunk,
        ),
        out_shape=[jax.ShapeDtypeStruct(packed, jnp.float32)] * window_slabs
        + [
            jax.ShapeDtypeStruct(gradient_matrix.shape, jnp.bfloat16),
            jax.ShapeDtypeStruct(orbitals.shape, jnp.bfloat16),
        ],
        in_specs=[HBM] * 7,
        out_specs=[VMEM] * (window_slabs + 2),
        compiler_params=pltpu.CompilerParams(vmem_limit_bytes=FORCE_MIB << 20),
        scratch_shapes=[
            pltpu.VMEM((1, nodes), jnp.float32),
            pltpu.VMEM(proj_values.shape, jnp.bfloat16),
            pltpu.VMEM((rows, parts, projs, nodes), jnp.bfloat16),
            pltpu.VMEM((window_slabs * atoms + 1, parts * projs, orbs), jnp.float32),
            pltpu.SMEM((rows,), jnp.int32),
            pltpu.SMEM((rows,), jnp.int32),
            pltpu.SMEM((cells,), jnp.float32),
            pltpu.SemaphoreType.DMA((parts + rows // chunk + 1,)),
            pltpu.SemaphoreType.DMA((3,)),
        ],
        cost_estimate=pl.CostEstimate(
            flops=flops, bytes_accessed=2 * orbitals.size + 2 * proj_values.size, transcendentals=0
        ),
        name="window_sums",
    )(
        *(
            pltpu.with_memory_space_constraint(operand, pltpu.HBM)
            for operand in (
                support_cell,
                support_atom,
                cell_scale,
                quad_weights.reshape(1, nodes),
                proj_values,
                gradient_matrix,
                orbitals,
            )
        )
    )
    return results[:window_slabs], results[window_slabs], results[window_slabs + 1]


def stress_kernel(
    occ_ref,
    quad_ref,
    scale_ref,
    matrix_ref,
    orbitals_ref,
    out_ref,
    even,
    odd,
    weight_ref,
    sums,
    *,
    share,
    block,
):
    orbs, nodes = weight_ref.shape
    cells = out_ref.shape[1]
    blocks = cells // block

    across = jnp.broadcast_to(occ_ref[...], (orbs, orbs))
    rows = lax.broadcasted_iota(jnp.int32, (orbs, orbs), 0)
    columns = lax.broadcasted_iota(jnp.int32, (orbs, orbs), 1)
    down = jnp.sum(jnp.where(rows == columns, across, 0.0), axis=1, keepdims=True)
    weight_ref[...] = down * quad_ref[...] * share

    def gradient_part(i, buffer, part, first=0, last=block):
        at = slice(part * nodes, (part + 1) * nodes)
        flat = orbitals_ref[pl.ds(i * block + first, last - first)]
        buffer[first * orbs : last * orbs, at] = jnp.dot(
            flat.reshape((last - first) * orbs, nodes),
            matrix_ref[:, at],
            preferred_element_type=jnp.float32,
        )

    def reduce_cells(buffer, first, last, totals):
        for cell in range(first, last):
            acc = [None] * len(PAIRS)
            for group in range(orbs // SUBLANES):
                at = slice(group * SUBLANES, (group + 1) * SUBLANES)
                row = cell * orbs + group * SUBLANES
                weight = weight_ref[at, :]
                grad = [
                    buffer[row : row + SUBLANES, i * nodes : (i + 1) * nodes] for i in range(3)
                ]
                scaled = [weight * grad[i] for i in range(3)]
                for k, (a, b) in enumerate(PAIRS):
                    term = scaled[a] * grad[b]
                    acc[k] = term if acc[k] is None else acc[k] + term
            for k in range(len(PAIRS)):
                lanes = acc[k][:, :LANES]
                for c in range(1, nodes // LANES):
                    lanes = lanes + acc[k][:, c * LANES : (c + 1) * LANES]
                totals[k].append(jnp.sum(lanes, axis=0, keepdims=True))

    def store(i, totals):
        at = pl.ds(pl.multiple_of(i * block, block), block)
        for k in range(len(PAIRS)):
            sums[k, at, :] = jnp.concatenate(totals[k], axis=0)

    def both(i, full, empty):
        totals = [[] for _ in PAIRS]
        for part in range(3):
            reduce_cells(full, part * block // 3, (part + 1) * block // 3, totals)
            gradient_part(i + 1, empty, part)
        store(i, totals)

    for part in range(3):
        gradient_part(0, even, part)

    def pair(t, carry):
        both(2 * t, even, odd)
        both(2 * t + 1, odd, even)
        return carry

    lax.fori_loop(0, blocks // 2 - 1, pair, 0)
    middle = block // 2
    before = [[] for _ in PAIRS]
    totals = [[] for _ in PAIRS]
    for part in range(3):
        reduce_cells(even, part * block // 3, (part + 1) * block // 3, before)
        gradient_part(blocks - 1, odd, part, 0, middle)
    store(blocks - 2, before)
    for part in range(3):
        reduce_cells(odd, part * middle // 3, (part + 1) * middle // 3, totals)
        gradient_part(blocks - 1, odd, part, middle, block)
    reduce_cells(odd, middle, block, totals)
    store(blocks - 1, totals)

    whole = [jnp.sum(jnp.transpose(sums[k]), axis=0, keepdims=True) for k in range(len(PAIRS))]
    half = 0.5 * (whole[0] + whole[1] + whole[2])
    square = scale_ref[...] * scale_ref[...]
    for k in range(3):
        out_ref[k : k + 1, :] = (half - whole[k]) * square
    for k in range(3, 6):
        out_ref[k : k + 1, :] = -whole[k] * square


def stress_sums(occupations, quad_weights, cell_scale, gradient_matrix, orbitals, orbital_total):
    cells, orbs, nodes = orbitals.shape
    block = min(1024 // orbs, cells // 2)
    columns = gradient_matrix.shape[1]
    return pl.pallas_call(
        functools.partial(stress_kernel, share=1.0 / orbital_total, block=block),
        out_shape=jax.ShapeDtypeStruct((6, cells), jnp.float32),
        in_specs=[VMEM, VMEM, VMEM, VMEM, VMEM],
        out_specs=VMEM,
        compiler_params=pltpu.CompilerParams(vmem_limit_bytes=STRESS_MIB << 20),
        scratch_shapes=[
            pltpu.VMEM((block * orbs, columns), jnp.float32),
            pltpu.VMEM((block * orbs, columns), jnp.float32),
            pltpu.VMEM((orbs, nodes), jnp.float32),
            pltpu.VMEM((6, cells, LANES), jnp.float32),
        ],
        cost_estimate=pl.CostEstimate(
            flops=2 * orbitals.size * columns, bytes_accessed=2 * orbitals.size, transcendentals=0
        ),
        name="stress_sums",
    )(
        occupations.reshape(1, orbs),
        quad_weights.reshape(1, nodes),
        cell_scale.reshape(1, cells),
        gradient_matrix,
        orbitals,
    )


def combine_kernel(*refs, windows):
    parts = refs[:windows]
    coupling_ref, occ_ref, stress_ref, out_ref = refs[windows:]
    atoms, high, _ = parts[0].shape
    orbs = occ_ref.shape[1]
    projs = coupling_ref.shape[1]
    components = high * LANES // orbs // projs - 1
    slab = lax.axis_index("cells")
    share = coupling_ref[pl.ds(pl.multiple_of(slab * atoms, atoms), atoms), :]
    down = jnp.transpose(share)
    rows = [[] for _ in range(components)]
    for atom in range(atoms):
        total = parts[0][atom]
        for part in parts[1:]:
            total = total + part[atom]
        whole = jnp.concatenate(
            [total[:, k * orbs : (k + 1) * orbs] for k in range(LANES // orbs)], axis=0
        )
        margin = whole[:projs] * (down[:, atom : atom + 1] * occ_ref[...])
        for i in range(components):
            deriv = whole[(i + 1) * projs : (i + 2) * projs]
            rows[i].append(jnp.sum(margin * deriv, axis=0, keepdims=True))
    lane = lax.broadcasted_iota(jnp.int32, (atoms, LANES), 1)
    line = lax.broadcasted_iota(jnp.int32, (atoms, LANES), 0)
    out_ref[...] = jnp.zeros_like(out_ref)
    out_ref[: stress_ref.shape[0], :] = stress_ref[...]
    for i in range(components):
        force = -2.0 * jnp.sum(jnp.concatenate(rows[i], axis=0), axis=1, keepdims=True)
        out_ref[SUBLANES + i : SUBLANES + i + 1, :LANES] = jnp.sum(
            jnp.where(lane == line, force, 0.0), axis=0, keepdims=True
        )


def combine(parts, proj_coupling, occupations, stress_part, slab_total):
    return pl.pallas_call(
        functools.partial(combine_kernel, windows=len(parts)),
        out_shape=jax.ShapeDtypeStruct((2 * SUBLANES, stress_part.shape[1]), jnp.float32),
        in_specs=[VMEM] * (len(parts) + 3),
        out_specs=VMEM,
        compiler_params=pltpu.CompilerParams(vmem_limit_bytes=8 << 20),
        name="combine",
    )(*parts, proj_coupling, occupations.reshape(1, -1), stress_part)


def add_kernel(*refs):
    stress_ref, force_ref = refs[-2:]
    total = refs[0][...]
    for ref in refs[1:-2]:
        total = total + ref[...]
    stress_ref[...] = total[: stress_ref.shape[0]]
    force_ref[...] = total[SUBLANES : SUBLANES + force_ref.shape[0], : force_ref.shape[1]]


def add_up(copies, atoms):
    return pl.pallas_call(
        add_kernel,
        out_shape=(
            jax.ShapeDtypeStruct((len(PAIRS), copies[0].shape[1]), jnp.float32),
            jax.ShapeDtypeStruct((3, atoms), jnp.float32),
        ),
        in_specs=[VMEM] * len(copies),
        out_specs=(VMEM, VMEM),
        compiler_params=pltpu.CompilerParams(vmem_limit_bytes=8 << 20),
        name="add_up",
    )(*copies)


def local(
    orbitals,
    gradient_matrix,
    quad_weights,
    cell_scale,
    occupations,
    support_cell,
    support_atom,
    proj_values,
    proj_coupling,
):
    cells, orbital_count, node_count = orbitals.shape
    atom_total = proj_coupling.shape[0]
    slab_total = lax.axis_size("cells")
    atom_share = atom_total // slab_total
    orbital_total = orbital_count * lax.axis_size("orb")

    parts, near_matrix, near_orbitals = window_sums(
        support_cell,
        support_atom,
        cell_scale,
        quad_weights,
        proj_values,
        gradient_matrix,
        orbitals,
        atom_share,
        slab_total,
    )
    received = [
        from_behind(parts[offset + REACH], "cells", offset) for offset in (2, 1, -1, -2)
    ]

    stress_part = stress_sums(
        occupations, quad_weights, cell_scale, near_matrix, near_orbitals, orbital_total
    )

    packed = combine(
        [parts[REACH]] + received, proj_coupling, occupations, stress_part, slab_total
    )
    size = lax.axis_size("orb")
    copies = [packed] + [
        lax.ppermute(packed, "orb", [(i, i ^ by) for i in range(size)]) for by in range(size - 1, 0, -1)
    ]
    return add_up(copies, atom_share)


def solution(mesh):
    return jax.shard_map(
        local,
        mesh=mesh,
        in_specs=(
            P("cells", "orb", None),
            P(),
            P(),
            P("cells"),
            P("orb"),
            P("cells"),
            P("cells"),
            P("cells", None, None),
            P(),
        ),
        out_specs=(P(None, "cells"), P(None, "cells")),
        check_vma=False,
    )
```
